768 devices in a mesh: replica: 24 (over z, y_lo), shard: 4 (over x), tensor: 8 (over y_hi, core).
Axes of the slice: x: 4, y: 8 (y_hi: 4, y_lo: 2; y = y_hi * 2 + y_lo), z: 12, core: 2. Of those that a mesh axis runs over, the one named last changes fastest.
Arguments:
- inputs: bfloat16 [12288, 8192], P(('replica', 'shard')), may hold values from -0.59765625 to 0.59765625
- gain: bfloat16 [8192], replicated, may hold values from 0.099609375 to 1.8984375
- value_weight: bfloat16 [8192, 2048], P('shard', 'tensor'), may hold values from -0.0625 to 0.0625
- value_cot: bfloat16 [12288, 2048], P(('replica', 'shard'), 'tensor'), may hold values from -0.5 to 0.5
- pseudo_grad: float32 [24, 2048, 3072], P('replica', ('shard', 'tensor')), may hold values from -6 to 6
- global_params: float32 [2048, 3072], P(('shard', 'tensor'), 'replica'), may hold values from -6 to 6
- momentum: float32 [2048, 3072], P(('shard', 'tensor'), 'replica'), may hold values from -3 to 3
Outputs:
- values: bfloat16 [12288, 2048], P(('replica', 'shard'), 'tensor')
- weight_grad: bfloat16 [24, 8192, 2048], P('replica', 'shard', 'tensor')
- input_grad: bfloat16 [12288, 8192], P(('replica', 'shard', 'tensor'))
- new_global: float32 [2048, 3072], P(('shard', 'tensor'), 'replica')
- new_momentum: float32 [2048, 3072], P(('shard', 'tensor'), 'replica')
The draws below stay inside these ranges and needn't reach their ends.
All inputs are finite; a program needn't handle non-finite values.
Results may differ from the reference program's by a relative error of at most 0.014.
Values may be sent and summed in bfloat16 or wider, within the bound.
No kernel may reach another device: no remote copies, remote signals or barrier semaphores. Data moves between devices by JAX's collectives and lax.ppermute only.
A program may use at most 64 MiB of HBM per device.

```python
import jax
import jax.numpy as jnp
from jax import lax

D = 8192
KVW = 2048
TOK_DEV = 128
TOKENS = 12288
FROWS = 2048
FCOLS = 3072
N_REPLICA = 24
N_SHARD = 4
N_TENSOR = 8


def raised(drawn, key, source, target, parts, factor):
    owner, partner = [(jnp.arange(drawn.shape[dim]) // (drawn.shape[dim] // parts)).reshape([-1 if axis == dim else 1 for axis in range(drawn.ndim)]) for dim in (source, target)]
    chosen = jax.random.permutation(key, parts)[partner]
    strong = (owner == chosen) | (owner == (partner + parts // 2) % parts)
    return jnp.where(strong, factor * drawn, drawn)


def steps_of(stream_key, shape, split, low, top_value):
    level, own = 1.0, jax.random.fold_in(stream_key, 6)
    for position, shards_of in split:
        draws = jnp.exp(jax.random.uniform(jax.random.fold_in(own, position), (shards_of,), jnp.float32, low / len(split), top_value / len(split)))
        level = level * jnp.repeat(draws, shape[position] // shards_of).reshape([-1 if axis == position else 1 for axis in range(len(shape))])
    return level


def centred(own_key, dims, scale, limit, pieces=(), held_as=jnp.bfloat16):
    loudness = steps_of(own_key, dims, pieces, -0.22, 0.18) if pieces else 1.0
    entries = jax.random.normal(own_key, dims, jnp.float32) * scale * loudness
    return jnp.minimum(jnp.maximum(entries, -limit), limit).astype(held_as)


def bell_draw_with(stream_key, shape, deviation, bound, pieces, heavy, held_as=jnp.bfloat16):
    array = deviation * jax.random.normal(stream_key, shape, jnp.float32)
    if pieces:
        array = array * steps_of(stream_key, shape, pieces, -0.22, 0.18)
    return jnp.clip(raised(array, jax.random.fold_in(stream_key, 3), *heavy), -bound, bound).astype(held_as)


def setup_inputs(seed: int = 0) -> dict:
    keys = jax.random.split(jax.random.key(seed), 8)
    return {
        "inputs": centred(keys[0], (TOKENS, D), 0.1, 0.59765625, ((0, 96),)),
        "gain": jnp.clip(1.0 + 0.18 * jax.random.normal(keys[1], (D,), jnp.float32), 0.099609375, 1.8984375).astype(jnp.bfloat16),
        "value_weight": centred(keys[2], (D, KVW), D ** -0.5, 0.0625, ((0, 4), (1, 8))),
        "value_cot": centred(keys[3], (TOKENS, KVW), TOK_DEV ** -0.5, 0.5, ((0, 96), (1, 8))),
        "pseudo_grad": bell_draw_with(keys[4], (N_REPLICA, FROWS, FCOLS), 1.0, 6.0, ((0, 24), (1, 32)), (0, 2, 24, 2.25), jnp.float32),
        "global_params": centred(keys[5], (FROWS, FCOLS), 1.0, 6.0, ((0, 32), (1, 24)), jnp.float32),
        "momentum": centred(keys[6], (FROWS, FCOLS), 0.5, 3.0, ((0, 32), (1, 24)), jnp.float32),
    }


norm_epsilon = 1e-05
outer_rate = 0.7
outer_beta = 0.9

def reference(inputs, gain, value_weight, value_cot, pseudo_grad, global_params, momentum):
    model_width = inputs.shape[1]
    value_cols = value_weight.shape[1]
    group_rows = TOK_DEV * N_SHARD
    block_cols = value_cols // N_TENSOR
    replica_inputs = inputs.reshape(N_REPLICA, group_rows, model_width)
    replica_cots = value_cot.reshape(N_REPLICA, group_rows, value_cols)
    gain_wide = gain.astype(jnp.float32)
    weight_blocks = value_weight.astype(jnp.float32).reshape(model_width, N_TENSOR, block_cols)

    def one_replica(operands):
        local_inputs, local_cot = operands
        wide_inputs = local_inputs.astype(jnp.float32)
        inv_scale = lax.rsqrt(lax.optimization_barrier(jnp.mean(wide_inputs * wide_inputs, axis=1, keepdims=True)) + norm_epsilon)
        normed = (wide_inputs * inv_scale * gain_wide).astype(jnp.bfloat16)
        values = jnp.dot(normed, value_weight, preferred_element_type=jnp.float32).astype(jnp.bfloat16)
        normed_wide = normed.astype(jnp.float32).reshape(N_SHARD, TOK_DEV, model_width)
        cot_wide = local_cot.astype(jnp.float32)
        cot_shards = cot_wide.reshape(N_SHARD, TOK_DEV, value_cols)
        partials = jnp.einsum('std,stk->sdk', normed_wide, cot_shards)
        partials = lax.optimization_barrier(partials.astype(jnp.bfloat16)).astype(jnp.float32)
        weight_grad = lax.optimization_barrier(jnp.sum(partials, axis=0)).astype(jnp.bfloat16)
        cot_blocks = cot_wide.reshape(group_rows, N_TENSOR, block_cols)
        hidden_parts = jnp.einsum('gtk,dtk->tgd', cot_blocks, weight_blocks)
        hidden_parts = lax.optimization_barrier(hidden_parts.astype(jnp.bfloat16)).astype(jnp.float32)
        hidden_grad = lax.optimization_barrier(jnp.sum(hidden_parts, axis=0))
        scaled = gain_wide * hidden_grad
        inner_mean = lax.optimization_barrier(jnp.mean(wide_inputs * scaled, axis=1, keepdims=True))
        cubed = inv_scale * inv_scale * inv_scale
        input_grad = (inv_scale * scaled - wide_inputs * cubed * inner_mean).astype(jnp.bfloat16)
        return (values, weight_grad, input_grad)
    values, weight_grad, input_grad = lax.map(one_replica, (replica_inputs, replica_cots))
    values = values.reshape(-1, value_cols)
    input_grad = input_grad.reshape(-1, model_width)
    average = lax.optimization_barrier(jnp.sum(pseudo_grad, axis=0)) / N_REPLICA
    new_momentum = outer_beta * momentum + average
    new_global = global_params - outer_rate * (average + outer_beta * new_momentum)
    return (values, weight_grad, input_grad, new_global, new_momentum)
```

```python
import jax
import jax.numpy as jnp
from jax import lax
from jax.sharding import PartitionSpec as P

norm_epsilon = 1e-05
outer_rate = 0.7
outer_beta = 0.9
CORES = 2


def body(inputs, gain, value_weight, value_cot, pseudo_grad, global_params, momentum):
    shards = lax.axis_size("shard")
    tensors = lax.axis_size("tensor")
    replicas = lax.axis_size("replica")
    tokens, width = inputs.shape
    block_rows, block_cols = value_weight.shape
    half = block_rows // CORES
    tensor = lax.axis_index("tensor")
    core = tensor % CORES
    swap = [(i, i ^ 1) for i in range(tensors)]
    near = [
        [s * tensors + h * CORES + c for s in range(shards) for c in range(CORES)]
        for h in range(tensors // CORES)
    ]
    group = ("shard", "tensor")
    fan = shards * CORES

    halves = value_weight.reshape(CORES, half, block_cols)
    kept = lax.dynamic_index_in_dim(halves, core, 0, keepdims=False)
    given = lax.dynamic_index_in_dim(halves, 1 - core, 0, keepdims=False)
    with jax.named_scope("wswap"):
        taken = lax.ppermute(given, "tensor", swap)
    weight = jnp.where(
        core == 0,
        jnp.concatenate([kept, taken], axis=1),
        jnp.concatenate([taken, kept], axis=1),
    )

    with jax.named_scope("cotgather"):
        cots = lax.all_to_all(
            jnp.broadcast_to(value_cot, (fan, tokens, block_cols)),
            group, 0, 0, axis_index_groups=near, tiled=True,
        )
    cot = cots.reshape(shards, CORES, tokens, block_cols).transpose(0, 2, 1, 3)
    cot = cot.reshape(shards * tokens, CORES * block_cols)

    wide_inputs = inputs.astype(jnp.float32)
    inv_scale = lax.rsqrt(jnp.mean(wide_inputs * wide_inputs, axis=1, keepdims=True) + norm_epsilon)
    gain_wide = gain.astype(jnp.float32)
    normed = (wide_inputs * inv_scale * gain_wide).astype(jnp.bfloat16)
    parts = lax.dynamic_index_in_dim(
        normed.reshape(tokens, shards, CORES, half), core, 2, keepdims=False
    ).transpose(1, 0, 2)
    with jax.named_scope("normed"):
        block = lax.all_to_all(parts, "shard", 0, 0, tiled=True)
    block = block.reshape(shards * tokens, half)

    hidden = lax.dot_general(
        cot, weight, (((1,), (1,)), ((), ())), preferred_element_type=jnp.float32
    ).astype(jnp.bfloat16)
    rows = tokens // tensors
    with jax.named_scope("hidden"):
        pieces = lax.all_to_all(
            hidden.reshape(shards * tensors, rows, half), group, 0, 0, tiled=True
        )

    local_grad = pseudo_grad[0].astype(jnp.bfloat16)
    frows, fcols = local_grad.shape
    own_cols = fcols // replicas
    with jax.named_scope("outer"):
        grads = lax.all_to_all(
            local_grad.reshape(frows, replicas, own_cols).transpose(1, 0, 2),
            "replica", 0, 0, tiled=True,
        )

    partial_values = jnp.dot(block, weight, preferred_element_type=jnp.float32).astype(jnp.bfloat16)
    sent = partial_values.reshape(shards, tokens, CORES, block_cols).transpose(0, 2, 1, 3)
    with jax.named_scope("values"):
        got = lax.all_to_all(
            sent.reshape(fan, tokens, block_cols), group, 0, 0, axis_index_groups=near, tiled=True
        )
    values = jnp.sum(got.astype(jnp.float32), axis=0).astype(jnp.bfloat16)

    wgrad = lax.dot_general(
        block, cot, (((0,), (0,)), ((), ())), preferred_element_type=jnp.float32
    ).astype(jnp.bfloat16)
    wgrad = wgrad.reshape(half, CORES, block_cols)
    mine = lax.dynamic_index_in_dim(wgrad, core, 1, keepdims=False)
    other = lax.dynamic_index_in_dim(wgrad, 1 - core, 1, keepdims=False)
    with jax.named_scope("gswap"):
        back = lax.ppermute(other, "tensor", swap)
    weight_grad = jnp.where(
        core == 0, jnp.stack([mine, back]), jnp.stack([back, mine])
    ).reshape(1, block_rows, block_cols)

    summed = jnp.sum(
        pieces.reshape(shards, tensors // CORES, CORES, rows, half).astype(jnp.float32), axis=1
    )
    summed = summed.transpose(2, 0, 1, 3).reshape(rows, width)
    first_row = tensor * rows
    input_rows = lax.dynamic_slice_in_dim(inputs, first_row, rows, 0).astype(jnp.float32)
    scale_rows = lax.dynamic_slice_in_dim(inv_scale, first_row, rows, 0)
    scaled = gain_wide * summed
    inner_mean = jnp.mean(input_rows * scaled, axis=1, keepdims=True)
    cubed = scale_rows * scale_rows * scale_rows
    input_grad = (scale_rows * scaled - input_rows * cubed * inner_mean).astype(jnp.bfloat16)

    average = jnp.sum(grads.reshape(replicas, frows, own_cols).astype(jnp.float32), axis=0) / replicas
    new_momentum = outer_beta * momentum + average
    new_global = global_params - outer_rate * (average + outer_beta * new_momentum)
    return (values, weight_grad, input_grad, new_global, new_momentum)


def solution(mesh):
    placed = (
        P(("replica", "shard"), None),
        P(),
        P("shard", "tensor"),
        P(("replica", "shard"), "tensor"),
        P("replica", ("shard", "tensor"), None),
        P(("shard", "tensor"), "replica"),
        P(("shard", "tensor"), "replica"),
    )
    return jax.shard_map(
        body,
        mesh=mesh,
        in_specs=placed,
        out_specs=(
            P(("replica", "shard"), "tensor"),
            P("replica", "shard", "tensor"),
            P(("replica", "shard", "tensor"), None),
            P(("shard", "tensor"), "replica"),
            P(("shard", "tensor"), "replica"),
        ),
        check_vma=False,
    )
```

```python
import functools

import jax
import jax.numpy as jnp
from jax import lax
from jax.experimental import pallas as pl
from jax.experimental.pallas import tpu as pltpu
from jax.sharding import PartitionSpec as P

norm_epsilon = 1e-05
outer_rate = 0.7
outer_beta = 0.9
CORES = 2
SHARDS = 4
CHIPS = 4
F32 = jnp.float32
BF16 = jnp.bfloat16


def cost(flops, moved):
    return pl.CostEstimate(flops=flops, bytes_accessed=moved, transcendentals=0)


def whole(shape):
    return pl.BlockSpec(shape, lambda *_: (0,) * len(shape))


def spread_kernel(x_ref, o_ref):
    for i in range(o_ref.shape[0]):
        o_ref[i] = x_ref[...]


def pack_kernel(idx, x_ref, g_ref, o0, o1, o2, o3, inv_ref):
    width = x_ref.shape[1]
    part = width // SHARDS
    chunk = 1024
    total = jnp.zeros((x_ref.shape[0], chunk), F32)
    for q in range(width // chunk):
        wide = x_ref[:, q * chunk:(q + 1) * chunk].astype(F32)
        total += wide * wide
    inv = lax.rsqrt(jnp.sum(total, axis=1, keepdims=True) / width + norm_epsilon)
    inv_ref[...] = jnp.broadcast_to(inv, inv_ref.shape)
    for k, out in enumerate((o0, o1, o2, o3)):
        begin = pl.multiple_of(lax.rem(idx[2] + k, SHARDS) * part, part)
        for q in range(part // chunk):
            at = pl.ds(begin + q * chunk, chunk)
            wide = x_ref[:, at].astype(F32)
            out[:, q * chunk:(q + 1) * chunk] = (wide * inv * g_ref[:, at]).astype(BF16)


def hidden_kernel(idx, cots, w_ref, v_ref, o0, o1, o2, o3, own, oth):
    core, chip = idx[0], idx[1]

    @pl.when(pl.program_id(0) == 0)
    def _():
        for j in range(CHIPS):
            row = pl.multiple_of((CORES * lax.rem(chip + j, CHIPS) + core) * 16, 16)
            for s in range(SHARDS):
                to = pl.ds(j * 64 + s * 16, 16)
                own[to, :] = cots[CORES * s + core, pl.ds(row, 16), :]
                oth[to, :] = cots[CORES * s + 1 - core, pl.ds(row, 16), :]

    dims = (((1,), (1,)), ((), ()))
    product = lax.dot_general(own[...], w_ref[...], dims, preferred_element_type=F32)
    product += lax.dot_general(oth[...], v_ref[...], dims, preferred_element_type=F32)
    for j, out in enumerate((o0, o1, o2, o3)):
        out[...] = product[j * 64:(j + 1) * 64].astype(BF16)


def values_kernel(n0, n1, n2, n3, w_ref, o0, o1, o2, o3, acc):
    step = pl.program_id(0)

    @pl.when(step == 0)
    def _():
        acc[...] = jnp.zeros_like(acc)

    for k, block in enumerate((n0, n1, n2, n3)):
        acc[k] += jnp.dot(block[...], w_ref[...], preferred_element_type=F32)

    @pl.when(step == pl.num_programs(0) - 1)
    def _():
        for k, out in enumerate((o0, o1, o2, o3)):
            out[...] = acc[k].astype(out.dtype)


def wgrad_kernel(idx, n0, n1, n2, n3, cots, o_ref):
    total = None
    for k, block in enumerate((n0, n1, n2, n3)):
        owner = lax.rem(idx[2] + SHARDS - k, SHARDS)
        term = lax.dot_general(
            block[...], cots[CORES * owner + idx[0]], (((0,), (0,)), ((), ())),
            preferred_element_type=F32,
        )
        total = term if total is None else total + term
    o_ref[0] = total.astype(BF16)


def merge_kernel(idx, h0, r1, r2, r3, v1, v2, v3, keep, m1, m2, m3):
    cols = m1.shape[1]
    tokens = v1.shape[0]
    for k, out in enumerate((keep, m1, m2, m3)):
        at = pl.ds(pl.multiple_of(lax.rem(idx[2] + k, SHARDS) * 16, 16), 16)
        for q in range(h0.shape[1] // cols):
            lanes = slice(q * cols, (q + 1) * cols)
            total = h0[at, lanes].astype(F32) + r1[at, lanes].astype(F32)
            total += r2[at, lanes].astype(F32) + r3[at, lanes].astype(F32)
            if k == 0:
                out[:, lanes] = total
            else:
                out[q * 16:(q + 1) * 16, :] = total.astype(BF16)
    for k, out, val in ((1, m1, v3), (2, m2, v2), (3, m3, v1)):
        out[tokens:, :] = val[...]


def final_kernel(idx, keep, m1, m2, m3, v0, x_ref, inv_ref, g_ref, o_ref, val_ref):
    part = keep.shape[1]
    tokens, cols = v0.shape
    width = x_ref.shape[1]
    inv = inv_ref[:, :1]
    places = []
    for k, got in enumerate((keep, m1, m2, m3)):
        begin = pl.multiple_of(lax.rem(idx[2] + SHARDS - k, SHARDS) * part, part)
        for q in range(part // cols):
            places.append((k, got, q, pl.ds(begin + q * cols, cols)))

    def scaled(k, got, q, at):
        if k == 0:
            term = got[:, q * cols:(q + 1) * cols]
        else:
            term = got[q * 16:(q + 1) * 16, :].astype(F32)
        return g_ref[:, at] * term

    total = jnp.zeros((16, cols), F32)
    for place in places:
        total += x_ref[:, place[3]].astype(F32) * scaled(*place)
    mean = jnp.sum(total, axis=1, keepdims=True) / width
    factor = inv * inv * inv * mean
    for place in places:
        at = place[3]
        o_ref[:, at] = (inv * scaled(*place) - x_ref[:, at].astype(F32) * factor).astype(BF16)
    summed = v0[...]
    for got in (m1, m2, m3):
        summed += got[tokens:, :].astype(F32)
    val_ref[...] = summed.astype(BF16)


def outer_pack_kernel(x_ref, o_ref):
    cols = o_ref.shape[2]
    for r in range(o_ref.shape[0]):
        o_ref[r] = x_ref[0, :, r * cols:(r + 1) * cols].astype(BF16)


def outer_kernel(g_ref, p_ref, m_ref, new_p, new_m):
    replicas = g_ref.shape[0]
    total = g_ref[0].astype(F32)
    for r in range(1, replicas):
        total += g_ref[r].astype(F32)
    average = total / replicas
    momentum = outer_beta * m_ref[...] + average
    new_m[...] = momentum
    new_p[...] = p_ref[...] - outer_rate * (average + outer_beta * momentum)


def body(inputs, gain, value_weight, value_cot, pseudo_grad, global_params, momentum):
    tensors = lax.axis_size("tensor")
    replicas = lax.axis_size("replica")
    tokens, width = inputs.shape
    rows, cols = value_weight.shape
    tensor = lax.axis_index("tensor")
    shard = lax.axis_index("shard")
    idx = jnp.stack([tensor % CORES, tensor // CORES, shard, tensor]).astype(jnp.int32)
    swap = [(i, i ^ 1) for i in range(tensors)]
    chip_shift = lambda j: [
        (t, (t // CORES + j) % CHIPS * CORES + t % CORES) for t in range(tensors)
    ]
    shard_shift = lambda k: [(s, (s + k) % SHARDS) for s in range(SHARDS)]
    near = [
        [s * tensors + h * CORES + c for s in range(SHARDS) for c in range(CORES)]
        for h in range(CHIPS)
    ]
    fan = SHARDS * CORES
    spec = jax.ShapeDtypeStruct
    rest = (1, 3, 2)

    spread = pl.pallas_call(
        spread_kernel, out_shape=spec((fan, tokens, cols), BF16),
        cost_estimate=cost(0, 600_000), name="spread",
    )(value_cot)
    with jax.named_scope("cotgather"):
        cots = lax.all_to_all(
            spread, ("shard", "tensor"), 0, 0, axis_index_groups=near, tiled=True
        )
    with jax.named_scope("wswap"):
        other_weight = lax.ppermute(value_weight, "tensor", swap)

    gain_row = gain.astype(F32).reshape(1, width)
    part = width // SHARDS
    *sent, inv_scale = pl.pallas_call(
        pack_kernel,
        grid_spec=pltpu.PrefetchScalarGridSpec(
            num_scalar_prefetch=1, grid=(tokens // 16,),
            in_specs=[pl.BlockSpec((16, width), lambda i, _: (i, 0)), whole((1, width))],
            out_specs=[pl.BlockSpec((16, part), lambda i, _: (i, 0))] * SHARDS
            + [pl.BlockSpec((16, 128), lambda i, _: (i, 0))],
        ),
        out_shape=[spec((tokens, part), BF16)] * SHARDS + [spec((tokens, 128), F32)],
        cost_estimate=cost(6_000_000, 4_300_000), name="pack",
    )(idx, inputs, gain_row)
    normed = [sent[0], None, None, None]
    for k in rest:
        with jax.named_scope(f"normed{k}"):
            normed[k] = lax.ppermute(sent[k], "shard", shard_shift(k))

    step = 512
    outs = pl.pallas_call(
        hidden_kernel,
        grid_spec=pltpu.PrefetchScalarGridSpec(
            num_scalar_prefetch=1, grid=(rows // step,),
            in_specs=[whole((fan, tokens, cols))]
            + [pl.BlockSpec((step, cols), lambda i, _: (i, 0))] * 2,
            out_specs=[pl.BlockSpec((64, step), lambda i, _: (0, i))] * CHIPS,
            scratch_shapes=[pltpu.VMEM((256, cols), BF16)] * 2,
        ),
        out_shape=[spec((64, rows), BF16)] * CHIPS,
        cost_estimate=cost(540_000_000, 3_700_000), name="hiddenmm",
    )(idx, cots, value_weight, other_weight)
    hidden = [outs[0], None, None, None]
    for j in rest:
        with jax.named_scope(f"hidden{j}"):
            hidden[j] = lax.ppermute(outs[j], "tensor", chip_shift(j))

    frows, fcols = pseudo_grad.shape[1:]
    own_cols = fcols // replicas
    packed = pl.pallas_call(
        outer_pack_kernel, grid=(3,),
        in_specs=[pl.BlockSpec((1, frows, fcols // 3), lambda i: (0, 0, i))],
        out_specs=pl.BlockSpec((replicas // 3, frows, own_cols), lambda i: (i, 0, 0)),
        out_shape=spec((replicas, frows, own_cols), BF16),
        cost_estimate=cost(0, 1_200_000), name="outerpack",
    )(pseudo_grad)
    packed, _ = lax.optimization_barrier((packed, outs[0]))
    with jax.named_scope("outer"):
        grads = lax.all_to_all(packed, "replica", 0, 0, tiled=True)

    partial_values = pl.pallas_call(
        values_kernel,
        grid_spec=pltpu.PrefetchScalarGridSpec(
            num_scalar_prefetch=0, grid=(rows // step,),
            in_specs=[pl.BlockSpec((tokens, step), lambda i: (0, i))] * SHARDS
            + [pl.BlockSpec((step, cols), lambda i: (i, 0))],
            out_specs=[whole((tokens, cols))] * SHARDS,
            scratch_shapes=[pltpu.VMEM((SHARDS, tokens, cols), F32)],
        ),
        out_shape=[spec((tokens, cols), F32)] + [spec((tokens, cols), BF16)] * 3,
        cost_estimate=cost(540_000_000, 3_300_000), name="valuesmm",
    )(*normed, value_weight)

    weight_grad = pl.pallas_call(
        wgrad_kernel,
        grid_spec=pltpu.PrefetchScalarGridSpec(
            num_scalar_prefetch=1, grid=(rows // step,),
            in_specs=[pl.BlockSpec((tokens, step), lambda i, _: (0, i))] * SHARDS
            + [whole((fan, tokens, cols))],
            out_specs=pl.BlockSpec((1, step, cols), lambda i, _: (0, i, 0)),
        ),
        out_shape=spec((1, rows, cols), BF16),
        cost_estimate=cost(540_000_000, 3_600_000), name="wgradmm",
    )(idx, *normed, cots)

    keep, *merged = pl.pallas_call(
        merge_kernel,
        grid_spec=pltpu.PrefetchScalarGridSpec(
            num_scalar_prefetch=1, grid=(1,),
            in_specs=[whole((64, rows))] * CHIPS + [whole((tokens, cols))] * 3,
            out_specs=[whole((16, rows))] + [whole((2 * tokens, cols))] * 3,
        ),
        out_shape=[spec((16, rows), F32)] + [spec((2 * tokens, cols), BF16)] * 3,
        cost_estimate=cost(1_000_000, 1_700_000), name="merge",
    )(idx, *hidden, *partial_values[1:])
    got = [None] * SHARDS
    for k in rest:
        with jax.named_scope(f"last{k}"):
            got[k] = lax.ppermute(merged[k - 1], "shard", shard_shift(k))

    input_grad, values = pl.pallas_call(
        final_kernel,
        grid_spec=pltpu.PrefetchScalarGridSpec(
            num_scalar_prefetch=1, grid=(1,),
            in_specs=[whole((16, rows))] + [whole((2 * tokens, cols))] * 3
            + [
                whole((tokens, cols)),
                pl.BlockSpec((16, width), lambda i, at: (at[3], 0)),
                pl.BlockSpec((16, 128), lambda i, at: (at[3], 0)),
                whole((1, width)),
            ],
            out_specs=[whole((16, width)), whole((tokens, cols))],
        ),
        out_shape=[spec((16, width), BF16), spec((tokens, cols), BF16)],
        cost_estimate=cost(2_000_000, 1_500_000), name="final",
    )(idx, keep, *got[1:], partial_values[0], inputs, inv_scale, gain_row)

    new_global, new_momentum = pl.pallas_call(
        outer_kernel, out_shape=[spec(momentum.shape, F32)] * 2,
        cost_estimate=cost(500_000, 600_000), name="outerstep",
    )(grads, global_params, momentum)
    return (values, weight_grad, input_grad, new_global, new_momentum)


def solution(mesh):
    placed = (
        P(("replica", "shard"), None),
        P(),
        P("shard", "tensor"),
        P(("replica", "shard"), "tensor"),
        P("replica", ("shard", "tensor"), None),
        P(("shard", "tensor"), "replica"),
        P(("shard", "tensor"), "replica"),
    )
    return jax.shard_map(
        body,
        mesh=mesh,
        in_specs=placed,
        out_specs=(
            P(("replica", "shard"), "tensor"),
            P("replica", "shard", "tensor"),
            P(("replica", "shard", "tensor"), None),
            P(("shard", "tensor"), "replica"),
            P(("shard", "tensor"), "replica"),
        ),
        check_vma=False,
    )
```

```python
import jax
import jax.numpy as jnp
from jax import lax
from jax.experimental import pallas as pl
from jax.experimental.pallas import tpu as pltpu
from jax.sharding import PartitionSpec as P


norm_epsilon = 1e-05
outer_rate = 0.7
outer_beta = 0.9
CORES = 2
SHARDS = 4
CHIPS = 4
F32 = jnp.float32
BF16 = jnp.bfloat16


def cost(flops, moved):
    return pl.CostEstimate(flops=flops, bytes_accessed=moved, transcendentals=0)


def whole(shape):
    return pl.BlockSpec(shape, lambda *_: (0,) * len(shape))


def spread_kernel(x_ref, o_ref, sems):
    copies = [pltpu.make_async_copy(x_ref, o_ref.at[i], sems.at[i]) for i in range(o_ref.shape[0])]
    for copy in copies:
        copy.start()
    for copy in copies:
        copy.wait()


def pack_kernel(idx, x_ref, g_ref, o0, o1, o2, o3, inv_ref):
    width = x_ref.shape[1]
    part = width // SHARDS
    chunk = 512
    total = jnp.zeros((x_ref.shape[0], chunk), F32)
    for q in range(width // chunk):
        wide = x_ref[:, q * chunk:(q + 1) * chunk].astype(F32)
        total += wide * wide
    inv = lax.rsqrt(jnp.sum(total, axis=1, keepdims=True) / width + norm_epsilon)
    inv_ref[...] = jnp.broadcast_to(inv, inv_ref.shape)
    for k, out in enumerate((o0, o1, o2, o3)):
        begin = (idx[2] ^ k) * part
        for q in range(part // chunk):
            at = pl.ds(pl.multiple_of(begin + q * chunk, chunk), chunk)
            wide = x_ref[:, at].astype(F32)
            out[:, q * chunk:(q + 1) * chunk] = (wide * inv * g_ref[:, at]).astype(BF16)


def rows_kernel(idx, cots, own, oth):
    core, chip = idx[0], idx[1]
    for j in range(CHIPS):
        row = pl.multiple_of((CORES * (chip ^ j) + core) * 16, 16)
        for s in range(SHARDS):
            to = slice(j * 64 + s * 16, j * 64 + (s + 1) * 16)
            own[to, :] = cots[CORES * s + core, pl.ds(row, 16), :]
            oth[to, :] = cots[CORES * s + 1 - core, pl.ds(row, 16), :]


def merge_kernel(idx, h0, r1, r2, r3, v1, v2, v3, keep, m1, m2, m3):
    cols = m1.shape[1]
    tokens = v1.shape[0]
    for k, out in enumerate((keep, m1, m2, m3)):
        at = pl.ds(pl.multiple_of((idx[2] ^ k) * 16, 16), 16)
        for q in range(h0.shape[1] // cols):
            lanes = slice(q * cols, (q + 1) * cols)
            total = h0[at, lanes].astype(F32) + r1[at, lanes].astype(F32)
            total += r2[at, lanes].astype(F32) + r3[at, lanes].astype(F32)
            if k == 0:
                out[:, lanes] = total
            else:
                out[q * 16:(q + 1) * 16, :] = total.astype(BF16)
    for out, val in ((m1, v1), (m2, v2), (m3, v3)):
        out[tokens:, :] = val[...]


def final_kernel(idx, keep, m1, m2, m3, v0, x_ref, inv_ref, g_ref, o_ref, val_ref):
    part = keep.shape[1]
    tokens, cols = v0.shape
    width = x_ref.shape[1]
    inv = inv_ref[:, :1]
    places = []
    for k, got in enumerate((keep, m1, m2, m3)):
        begin = (idx[2] ^ k) * part
        for q in range(part // cols):
            at = pl.ds(pl.multiple_of(begin + q * cols, cols), cols)
            places.append((k, got, q, at))

    def scaled(k, got, q, at):
        if k == 0:
            term = got[:, q * cols:(q + 1) * cols]
        else:
            term = got[q * 16:(q + 1) * 16, :].astype(F32)
        return g_ref[:, at] * term

    total = jnp.zeros((16, cols), F32)
    for place in places:
        total += x_ref[:, place[3]].astype(F32) * scaled(*place)
    mean = jnp.sum(total, axis=1, keepdims=True) / width
    factor = inv * inv * inv * mean
    for place in places:
        at = place[3]
        o_ref[:, at] = (inv * scaled(*place) - x_ref[:, at].astype(F32) * factor).astype(BF16)
    summed = v0[...]
    for got in (m1, m2, m3):
        summed += got[tokens:, :].astype(F32)
    val_ref[...] = summed.astype(BF16)


def outer_pack_kernel(x_ref, o_ref):
    cols = o_ref.shape[2]
    for r in range(o_ref.shape[0]):
        o_ref[r] = x_ref[0, :, r * cols:(r + 1) * cols].astype(BF16)


def outer_kernel(g_ref, p_ref, m_ref, new_p, new_m):
    replicas = g_ref.shape[0]
    total = g_ref[0].astype(F32)
    for r in range(1, replicas):
        total += g_ref[r].astype(F32)
    average = total / replicas
    momentum = outer_beta * m_ref[...] + average
    new_m[...] = momentum
    new_p[...] = p_ref[...] - outer_rate * (average + outer_beta * momentum)


def body(inputs, gain, value_weight, value_cot, pseudo_grad, global_params, momentum):
    tensors = lax.axis_size("tensor")
    replicas = lax.axis_size("replica")
    tokens, width = inputs.shape
    rows, cols = value_weight.shape
    tensor = lax.axis_index("tensor")
    shard = lax.axis_index("shard")
    idx = jnp.stack([tensor % CORES, tensor // CORES, shard, tensor]).astype(jnp.int32)
    swap = [(i, i ^ 1) for i in range(tensors)]
    chip_shift = lambda j: [
        (t, (t // CORES ^ j) * CORES + t % CORES) for t in range(tensors)
    ]
    shard_shift = lambda k: [(s, s ^ k) for s in range(SHARDS)]
    near = [
        [s * tensors + h * CORES + c for s in range(SHARDS) for c in range(CORES)]
        for h in range(CHIPS)
    ]
    fan = SHARDS * CORES
    spec = jax.ShapeDtypeStruct
    rest = (1, 3, 2)

    spread = pl.pallas_call(
        spread_kernel, out_shape=spec((fan, tokens, cols), BF16),
        in_specs=[pl.BlockSpec(memory_space=pltpu.VMEM)],
        out_specs=pl.BlockSpec(memory_space=pl.ANY),
        scratch_shapes=[pltpu.SemaphoreType.DMA((fan,))],
        cost_estimate=cost(0, 600_000), name="spread",
    )(value_cot)
    cots = lax.all_to_all(
        spread, ("shard", "tensor"), 0, 0, axis_index_groups=near, tiled=True
    )
    other_weight = lax.ppermute(value_weight, "tensor", swap)

    gain_row = gain.astype(F32).reshape(1, width)
    part = width // SHARDS
    packing = pl.pallas_call(
        pack_kernel,
        grid_spec=pltpu.PrefetchScalarGridSpec(
            num_scalar_prefetch=1, grid=(tokens // 16,),
            in_specs=[pl.BlockSpec((16, width), lambda i, _: (i, 0)), whole((1, width))],
            out_specs=[pl.BlockSpec((16, part), lambda i, _: (i, 0))] * SHARDS
            + [pl.BlockSpec((16, 128), lambda i, _: (i, 0))],
        ),
        out_shape=[spec((tokens, part), BF16)] * SHARDS + [spec((tokens, 128), F32)],
        cost_estimate=cost(6_000_000, 4_300_000), name="pack",
    )
    *sent, inv_scale = packing(idx, inputs, gain_row)
    normed = [sent[0], None, None, None]
    for k in rest:
        normed[k] = lax.ppermute(sent[k], "shard", shard_shift(k))

    own_rows, other_rows = pl.pallas_call(
        rows_kernel,
        grid_spec=pltpu.PrefetchScalarGridSpec(
            num_scalar_prefetch=1, grid=(1,),
            in_specs=[whole((fan, tokens, cols))],
            out_specs=[whole((256, cols))] * 2,
        ),
        out_shape=[spec((256, cols), BF16)] * 2,
        cost_estimate=cost(0, 800_000), name="rows",
    )(idx, cots)
    last_dims = (((1,), (1,)), ((), ()))
    product = lax.dot_general(own_rows, value_weight, last_dims, preferred_element_type=F32)
    product += lax.dot_general(other_rows, other_weight, last_dims, preferred_element_type=F32)
    product = product.astype(BF16)
    outs = [product[j * 64:(j + 1) * 64] for j in range(CHIPS)]
    hidden = [outs[0], None, None, None]
    for j in rest:
        hidden[j] = lax.ppermute(outs[j], "tensor", chip_shift(j))

    frows, fcols = pseudo_grad.shape[1:]
    own_cols = fcols // replicas
    outer_packing = pl.pallas_call(
        outer_pack_kernel, grid=(3,),
        in_specs=[pl.BlockSpec((1, frows, fcols // 3), lambda i: (0, 0, i))],
        out_specs=pl.BlockSpec((replicas // 3, frows, own_cols), lambda i: (i, 0, 0)),
        out_shape=spec((replicas, frows, own_cols), BF16),
        cost_estimate=cost(0, 1_200_000), name="outerpack",
    )
    packed = outer_packing(pseudo_grad)
    grads = lax.all_to_all(packed, "replica", 0, 0, tiled=True)

    partial_values = [
        jnp.dot(block, value_weight, preferred_element_type=F32) for block in normed
    ]
    partial_values[1:] = [part.astype(BF16) for part in partial_values[1:]]

    own_cots = [
        lax.dynamic_index_in_dim(cots, CORES * (shard ^ k) + tensor % CORES, 0, keepdims=False)
        for k in range(SHARDS)
    ]
    weight_grad = lax.dot_general(
        jnp.concatenate(normed, axis=0), jnp.concatenate(own_cots, axis=0),
        (((0,), (0,)), ((), ())), preferred_element_type=F32,
    ).astype(BF16)[None]

    keep, *merged = pl.pallas_call(
        merge_kernel,
        grid_spec=pltpu.PrefetchScalarGridSpec(
            num_scalar_prefetch=1, grid=(1,),
            in_specs=[whole((64, rows))] * CHIPS + [whole((tokens, cols))] * 3,
            out_specs=[whole((16, rows))] + [whole((2 * tokens, cols))] * 3,
        ),
        out_shape=[spec((16, rows), F32)] + [spec((2 * tokens, cols), BF16)] * 3,
        cost_estimate=cost(1_000_000, 1_700_000), name="merge",
    )(idx, *hidden, *partial_values[1:])
    got = [None] * SHARDS
    for k in rest:
        got[k] = lax.ppermute(merged[k - 1], "shard", shard_shift(k))

    input_grad, values = pl.pallas_call(
        final_kernel,
        grid_spec=pltpu.PrefetchScalarGridSpec(
            num_scalar_prefetch=1, grid=(1,),
            in_specs=[whole((16, rows))] + [whole((2 * tokens, cols))] * 3
            + [
                whole((tokens, cols)),
                pl.BlockSpec((16, width), lambda i, at: (at[3], 0)),
                pl.BlockSpec((16, 128), lambda i, at: (at[3], 0)),
                whole((1, width)),
            ],
            out_specs=[whole((16, width)), whole((tokens, cols))],
        ),
        out_shape=[spec((16, width), BF16), spec((tokens, cols), BF16)],
        cost_estimate=cost(2_000_000, 1_500_000), name="final",
    )(idx, keep, *got[1:], partial_values[0], inputs, inv_scale, gain_row)

    new_global, new_momentum = pl.pallas_call(
        outer_kernel, out_shape=[spec(momentum.shape, F32)] * 2,
        cost_estimate=cost(500_000, 600_000), name="outerstep",
    )(grads, global_params, momentum)
    return (values, weight_grad, input_grad, new_global, new_momentum)


def solution(mesh):
    placed = (
        P(("replica", "shard"), None),
        P(),
        P("shard", "tensor"),
        P(("replica", "shard"), "tensor"),
        P("replica", ("shard", "tensor"), None),
        P(("shard", "tensor"), "replica"),
        P(("shard", "tensor"), "replica"),
    )
    return jax.shard_map(
        body,
        mesh=mesh,
        in_specs=placed,
        out_specs=(
            P(("replica", "shard"), "tensor"),
            P("replica", "shard", "tensor"),
            P(("replica", "shard", "tensor"), None),
            P(("shard", "tensor"), "replica"),
            P(("shard", "tensor"), "replica"),
        ),
        check_vma=False,
    )
```

```python
import jax
import jax.numpy as jnp
from jax import lax
from jax.experimental import pallas as pl
from jax.experimental.pallas import tpu as pltpu
from jax.sharding import PartitionSpec as P


norm_epsilon = 1e-05
outer_rate = 0.7
outer_beta = 0.9
CORES = 2
SHARDS = 4
CHIPS = 4
F32 = jnp.float32
BF16 = jnp.bfloat16


def cost(flops, moved):
    return pl.CostEstimate(flops=flops, bytes_accessed=moved, transcendentals=0)


def whole(shape):
    return pl.BlockSpec(shape, lambda *_: (0,) * len(shape))


def block_of(idx, place, flip=0):
    return CORES * (idx[1] ^ (place % CHIPS)) + (idx[0] ^ flip ^ (place // CHIPS))


def spread_kernel(idx, x_ref, o_ref, both, sems):
    fan = o_ref.shape[0]
    copies = []
    for core in range(CORES):
        for place in range(2 * CHIPS):
            block = CORES * (idx[1] ^ (place % CHIPS)) + (core ^ (place // CHIPS))
            both[core, place * 16:(place + 1) * 16, :] = x_ref[pl.ds(pl.multiple_of(block * 16, 16), 16), :]
        for s in range(fan // CORES):
            at = CORES * s + core
            copies.append(pltpu.make_async_copy(both.at[core], o_ref.at[at], sems.at[at]))
            copies[-1].start()
    for copy in copies:
        copy.wait()


def pack_kernel(idx, x_ref, g_ref, o_ref, inv_ref, gain):
    @pl.when(pl.program_id(0) == 0)
    def _():
        gain[...] = g_ref[...].astype(F32)

    rows, width = x_ref.shape
    part = width // SHARDS
    total = jnp.zeros((rows, 512), F32)
    for q in range(width // 512):
        wide = x_ref[:, q * 512:(q + 1) * 512].astype(F32)
        total += wide * wide
    inv = lax.rsqrt(jnp.sum(total, axis=1, keepdims=True) / width + norm_epsilon)
    inv = jnp.broadcast_to(inv, inv_ref.shape)
    inv_ref[...] = inv
    for q in range(width // 128):
        wide = x_ref[:, q * 128:(q + 1) * 128].astype(F32)
        d, at = q * 128 // part, q * 128 % part
        o_ref[d, :, at:at + 128] = (wide * inv * gain[q:q + 1, :]).astype(BF16)


def merge_kernel(idx, h0, r1, r2, r3, values, keep, v0, m1, m2, m3):
    tokens, cols = v0.shape
    for k, out in enumerate((keep, m1, m2, m3)):
        at = pl.ds(pl.multiple_of((idx[2] ^ k) * 16, 16), 16)
        for q in range(h0.shape[1] // cols):
            lanes = slice(q * cols, (q + 1) * cols)
            total = h0[at, lanes].astype(F32) + r1[at, lanes].astype(F32)
            total += r2[at, lanes].astype(F32) + r3[at, lanes].astype(F32)
            if k == 0:
                out[:, lanes] = total
            else:
                out[q * 16:(q + 1) * 16, :] = total.astype(BF16)
    for k, out in enumerate((v0, m1, m2, m3)):
        val = values[pl.ds(pl.multiple_of((idx[2] ^ k) * tokens, tokens), tokens), :]
        if k == 0:
            out[...] = val
        else:
            out[tokens:, :] = val


def final_kernel(
    idx, keep, m1, m2, m3, v0, x_ref, inv_ref, g_ref, grads, p_ref, q_ref,
    o_ref, val_ref, new_p, new_m, gain,
):
    gain[...] = g_ref[...].astype(F32)
    part = keep.shape[1]
    tokens, cols = v0.shape
    width = x_ref.shape[1]
    lanes = 128
    inv = inv_ref[...]
    places = []
    for k, got in enumerate((keep, m1, m2, m3)):
        first = (idx[2] ^ k) * (part // lanes)
        for q in range(part // lanes):
            at = pl.ds(pl.multiple_of((first + q) * lanes, lanes), lanes)
            places.append((k, got, q, first + q, at))

    def scaled(k, got, q, row, at):
        if k == 0:
            term = got[:, q * lanes:(q + 1) * lanes]
        else:
            r, l = q * lanes // cols * 16, q * lanes % cols
            term = got[r:r + 16, l:l + lanes].astype(F32)
        return gain[pl.ds(row, 1), :] * term

    total = jnp.zeros((16, lanes), F32)
    for place in places:
        total += x_ref[:, place[4]].astype(F32) * scaled(*place)
    mean = jnp.sum(total, axis=1, keepdims=True) / width
    factor = inv * inv * inv * mean
    for place in places:
        at = place[4]
        o_ref[:, at] = (inv * scaled(*place) - x_ref[:, at].astype(F32) * factor).astype(BF16)
    for place in range(2 * CHIPS):
        rows = slice(place * 16, (place + 1) * 16)
        summed = v0[rows, :].astype(F32)
        for got in (m1, m2, m3):
            summed += got[tokens + place * 16:tokens + (place + 1) * 16, :].astype(F32)
        to = pl.ds(pl.multiple_of(block_of(idx, place) * 16, 16), 16)
        val_ref[to, :] = summed.astype(BF16)

    replicas = grads.shape[0]
    outer = grads[0].astype(F32)
    for r in range(1, replicas):
        outer += grads[r].astype(F32)
    average = outer / replicas
    momentum = outer_beta * q_ref[...] + average
    new_m[...] = momentum
    new_p[...] = p_ref[...] - outer_rate * (average + outer_beta * momentum)


def outer_pack_kernel(x_ref, o_ref):
    cols = o_ref.shape[2]
    for r in range(o_ref.shape[0]):
        o_ref[r] = x_ref[0, :, r * cols:(r + 1) * cols].astype(BF16)


def body(inputs, gain, value_weight, value_cot, pseudo_grad, global_params, momentum):
    tensors = lax.axis_size("tensor")
    replicas = lax.axis_size("replica")
    tokens, width = inputs.shape
    rows, cols = value_weight.shape
    tensor = lax.axis_index("tensor")
    shard = lax.axis_index("shard")
    idx = jnp.stack([tensor % CORES, tensor // CORES, shard, tensor]).astype(jnp.int32)
    swap = [(i, i ^ 1) for i in range(tensors)]
    chip_shift = lambda j: [
        (t, (t // CORES ^ j) * CORES + t % CORES) for t in range(tensors)
    ]
    shard_shift = lambda k: [(s, s ^ k) for s in range(SHARDS)]
    near = [
        [s * tensors + h * CORES + c for s in range(SHARDS) for c in range(CORES)]
        for h in range(CHIPS)
    ]
    fan = SHARDS * CORES
    spec = jax.ShapeDtypeStruct
    rest = (1, 3, 2)

    spread = pl.pallas_call(
        spread_kernel,
        grid_spec=pltpu.PrefetchScalarGridSpec(
            num_scalar_prefetch=1, grid=(1,),
            in_specs=[whole((tokens, cols))],
            out_specs=pl.BlockSpec(memory_space=pl.ANY),
            scratch_shapes=[pltpu.VMEM((CORES, tokens, cols), BF16), pltpu.SemaphoreType.DMA((fan,))],
        ),
        out_shape=spec((fan, tokens, cols), BF16),
        cost_estimate=cost(0, 600_000), name="spread",
    )(idx, value_cot)
    cots = lax.all_to_all(
        spread, ("shard", "tensor"), 0, 0, axis_index_groups=near, tiled=True
    )
    other_weight = lax.ppermute(value_weight, "tensor", swap)

    gains = gain.reshape(width // 128, 128)
    part = width // SHARDS
    packing = pl.pallas_call(
        pack_kernel,
        grid_spec=pltpu.PrefetchScalarGridSpec(
            num_scalar_prefetch=1, grid=(tokens // 16,),
            in_specs=[pl.BlockSpec((16, width), lambda i, _: (i, 0)), whole(gains.shape)],
            out_specs=[
                pl.BlockSpec(
                    (SHARDS, 16, part),
                    lambda i, at: (0, ((i // CORES) ^ at[1]) + CHIPS * ((i % CORES) ^ at[0]), 0),
                ),
                pl.BlockSpec((16, 128), lambda i, _: (i, 0)),
            ],
            scratch_shapes=[pltpu.VMEM(gains.shape, F32)],
        ),
        out_shape=[spec((SHARDS, tokens, part), BF16), spec((tokens, 128), F32)],
        cost_estimate=cost(6_000_000, 4_300_000), name="pack",
    )
    sent, inv_scale = packing(idx, inputs, gains)
    normed = lax.all_to_all(sent, "shard", 0, 0, tiled=True).reshape(SHARDS * tokens, part)

    pairs = cots.reshape(SHARDS, CORES, tokens, cols)
    own_cots = lax.dynamic_index_in_dim(pairs, tensor % CORES, 1, keepdims=False)
    other_cots = lax.dynamic_index_in_dim(pairs, 1 - tensor % CORES, 1, keepdims=False)
    share = tokens // CORES
    own_rows = own_cots[:, :share].reshape(SHARDS * share, cols)
    other_rows = other_cots[:, :share].reshape(SHARDS * share, cols)
    last_dims = (((1,), (1,)), ((), ()))
    product = lax.dot_general(own_rows, value_weight, last_dims, preferred_element_type=F32)
    product += lax.dot_general(other_rows, other_weight, last_dims, preferred_element_type=F32)
    product = product.astype(BF16).reshape(SHARDS, CHIPS, 16, rows)
    outs = [product[:, j].reshape(SHARDS * 16, rows) for j in range(CHIPS)]
    hidden = [outs[0], None, None, None]
    for j in rest:
        hidden[j] = lax.ppermute(outs[j], "tensor", chip_shift(j))

    frows, fcols = pseudo_grad.shape[1:]
    own_cols = fcols // replicas
    outer_packing = pl.pallas_call(
        outer_pack_kernel, grid=(3,),
        in_specs=[pl.BlockSpec((1, frows, fcols // 3), lambda i: (0, 0, i))],
        out_specs=pl.BlockSpec((replicas // 3, frows, own_cols), lambda i: (i, 0, 0)),
        out_shape=spec((replicas, frows, own_cols), BF16),
        cost_estimate=cost(0, 1_200_000), name="outerpack",
    )
    packed = outer_packing(pseudo_grad)
    grads = lax.all_to_all(packed, "replica", 0, 0, tiled=True)

    partial_values = jnp.dot(normed, value_weight, preferred_element_type=F32).astype(BF16)
    weight_grad = lax.dot_general(
        normed, own_cots.reshape(SHARDS * tokens, cols),
        (((0,), (0,)), ((), ())), preferred_element_type=F32,
    ).astype(BF16)[None]

    keep, own_values, *merged = pl.pallas_call(
        merge_kernel,
        grid_spec=pltpu.PrefetchScalarGridSpec(
            num_scalar_prefetch=1, grid=(1,),
            in_specs=[whole((64, rows))] * CHIPS + [whole((SHARDS * tokens, cols))],
            out_specs=[whole((16, rows)), whole((tokens, cols))] + [whole((2 * tokens, cols))] * 3,
        ),
        out_shape=[spec((16, rows), F32), spec((tokens, cols), BF16)]
        + [spec((2 * tokens, cols), BF16)] * 3,
        cost_estimate=cost(1_000_000, 1_700_000), name="merge",
    )(idx, *hidden, partial_values)
    got = [None] * SHARDS
    for k in rest:
        got[k] = lax.ppermute(merged[k - 1], "shard", shard_shift(k))

    input_grad, values, new_global, new_momentum = pl.pallas_call(
        final_kernel,
        grid_spec=pltpu.PrefetchScalarGridSpec(
            num_scalar_prefetch=1, grid=(1,),
            in_specs=[whole((16, rows))] + [whole((2 * tokens, cols))] * 3
            + [
                whole((tokens, cols)),
                pl.BlockSpec((16, width), lambda i, at: (at[3], 0)),
                pl.BlockSpec((16, 128), lambda i, at: (at[3], 0)),
                whole(gains.shape),
                whole(grads.shape),
                whole(momentum.shape),
                whole(momentum.shape),
            ],
            out_specs=[
                whole((16, width)), whole((tokens, cols)),
                whole(momentum.shape), whole(momentum.shape),
            ],
            scratch_shapes=[pltpu.VMEM(gains.shape, F32)],
        ),
        out_shape=[spec((16, width), BF16), spec((tokens, cols), BF16)]
        + [spec(momentum.shape, F32)] * 2,
        cost_estimate=cost(2_000_000, 2_100_000), name="final",
    )(idx, keep, *got[1:], own_values, inputs, inv_scale, gains, grads, global_params, momentum)
    return (values, weight_grad, input_grad, new_global, new_momentum)


def solution(mesh):
    placed = (
        P(("replica", "shard"), None),
        P(),
        P("shard", "tensor"),
        P(("replica", "shard"), "tensor"),
        P("replica", ("shard", "tensor"), None),
        P(("shard", "tensor"), "replica"),
        P(("shard", "tensor"), "replica"),
    )
    return jax.shard_map(
        body,
        mesh=mesh,
        in_specs=placed,
        out_specs=(
            P(("replica", "shard"), "tensor"),
            P("replica", "shard", "tensor"),
            P(("replica", "shard", "tensor"), None),
            P(("shard", "tensor"), "replica"),
            P(("shard", "tensor"), "replica"),
        ),
        check_vma=False,
    )
```

```python
import jax
import jax.numpy as jnp
from jax import lax
from jax.experimental import pallas as pl
from jax.experimental.pallas import tpu as pltpu
from jax.sharding import PartitionSpec as P


norm_epsilon = 1e-05
outer_rate = 0.7
outer_beta = 0.9
CORES = 2
SHARDS = 4
CHIPS = 4
F32 = jnp.float32
BF16 = jnp.bfloat16


def cost(flops, moved):
    return pl.CostEstimate(flops=flops, bytes_accessed=moved, transcendentals=0)


def whole(shape):
    return pl.BlockSpec(shape, lambda *_: (0,) * len(shape))


def block_of(idx, place):
    return CORES * (idx[1] ^ (place % CHIPS)) + place // CHIPS


def spread_kernel(idx, x_ref, o_ref, ordered, sems):
    for place in range(2 * CHIPS):
        at = pl.multiple_of(block_of(idx, place) * 16, 16)
        ordered[place * 16:(place + 1) * 16, :] = x_ref[pl.ds(at, 16), :]
    copies = [
        pltpu.make_async_copy(ordered, o_ref.at[i], sems.at[i]) for i in range(o_ref.shape[0])
    ]
    for copy in copies:
        copy.start()
    for copy in copies:
        copy.wait()


def inverse_scale(x_ref):
    rows, width = x_ref.shape
    total = jnp.zeros((rows, 512), F32)
    for q in range(width // 512):
        wide = x_ref[:, q * 512:(q + 1) * 512].astype(F32)
        total += wide * wide
    inv = lax.rsqrt(jnp.sum(total, axis=1, keepdims=True) / width + norm_epsilon)
    return jnp.broadcast_to(inv, (rows, 128))


def pack_kernel(idx, x_ref, g_ref, o_ref, gain):
    @pl.when(pl.program_id(0) == 0)
    def _():
        gain[...] = g_ref[...].astype(F32)

    width = x_ref.shape[1]
    part = width // SHARDS
    inv = inverse_scale(x_ref)
    half = part // CORES
    for d in range(SHARDS):
        for q in range(half // 128):
            row = (d * CORES + idx[0]) * (half // 128) + q
            wide = x_ref[:, pl.ds(pl.multiple_of(row * 128, 128), 128)].astype(F32)
            o_ref[d, :, q * 128:(q + 1) * 128] = (wide * inv * gain[pl.ds(row, 1), :]).astype(BF16)


def merge_kernel(idx, h0, r1, r2, r3, values, keep, v0, m1, m2, m3):
    tokens, cols = v0.shape
    for k, out in enumerate((keep, m1, m2, m3)):
        at = pl.ds(pl.multiple_of((idx[2] ^ k) * 16, 16), 16)
        for q in range(h0.shape[1] // cols):
            lanes = slice(q * cols, (q + 1) * cols)
            total = h0[at, lanes].astype(F32) + r1[at, lanes].astype(F32)
            total += r2[at, lanes].astype(F32) + r3[at, lanes].astype(F32)
            if k == 0:
                out[:, lanes] = total
            else:
                out[q * 16:(q + 1) * 16, :] = total.astype(BF16)
    for k, out in enumerate((v0, m1, m2, m3)):
        val = values[pl.ds(pl.multiple_of((idx[2] ^ k) * tokens, tokens), tokens), :]
        if k == 0:
            out[...] = val
        else:
            out[tokens:, :] = val


def final_kernel(
    idx, keep, m1, m2, m3, v0, x_ref, g_ref, grads, p_ref, q_ref,
    o_ref, val_ref, new_p, new_m, gain,
):
    gain[...] = g_ref[...].astype(F32)
    part = keep.shape[1]
    tokens, cols = v0.shape
    width = x_ref.shape[1]
    lanes = 128
    inv = inverse_scale(x_ref)
    places = []
    for k, got in enumerate((keep, m1, m2, m3)):
        first = (idx[2] ^ k) * (part // lanes)
        for q in range(part // lanes):
            at = pl.ds(pl.multiple_of((first + q) * lanes, lanes), lanes)
            places.append((k, got, q, first + q, at))

    def scaled(k, got, q, row, at):
        if k == 0:
            term = got[:, q * lanes:(q + 1) * lanes]
        else:
            r, l = q * lanes // cols * 16, q * lanes % cols
            term = got[r:r + 16, l:l + lanes].astype(F32)
        return gain[pl.ds(row, 1), :] * term

    total = jnp.zeros((16, lanes), F32)
    for place in places:
        total += x_ref[:, place[4]].astype(F32) * scaled(*place)
    mean = jnp.sum(total, axis=1, keepdims=True) / width
    factor = inv * inv * inv * mean
    for place in places:
        at = place[4]
        o_ref[:, at] = (inv * scaled(*place) - x_ref[:, at].astype(F32) * factor).astype(BF16)
    for place in range(2 * CHIPS):
        rows = slice(place * 16, (place + 1) * 16)
        summed = v0[rows, :].astype(F32)
        for got in (m1, m2, m3):
            summed += got[tokens + place * 16:tokens + (place + 1) * 16, :].astype(F32)
        to = pl.ds(pl.multiple_of(block_of(idx, place) * 16, 16), 16)
        val_ref[to, :] = summed.astype(BF16)

    replicas = grads.shape[0]
    outer = grads[0].astype(F32)
    for r in range(1, replicas):
        outer += grads[r].astype(F32)
    average = outer / replicas
    momentum = outer_beta * q_ref[...] + average
    new_m[...] = momentum
    new_p[...] = p_ref[...] - outer_rate * (average + outer_beta * momentum)


def outer_pack_kernel(x_ref, o_ref):
    cols = o_ref.shape[2]
    for r in range(o_ref.shape[0]):
        o_ref[r] = x_ref[0, :, r * cols:(r + 1) * cols].astype(BF16)


def body(inputs, gain, value_weight, value_cot, pseudo_grad, global_params, momentum):
    tensors = lax.axis_size("tensor")
    replicas = lax.axis_size("replica")
    tokens, width = inputs.shape
    rows, cols = value_weight.shape
    tensor = lax.axis_index("tensor")
    shard = lax.axis_index("shard")
    idx = jnp.stack([tensor % CORES, tensor // CORES, shard, tensor]).astype(jnp.int32)
    swap = [(i, i ^ 1) for i in range(tensors)]
    chip_shift = lambda j: [
        (t, (t // CORES ^ j) * CORES + t % CORES) for t in range(tensors)
    ]
    shard_shift = lambda k: [(s, s ^ k) for s in range(SHARDS)]
    near = [
        [s * tensors + h * CORES + c for s in range(SHARDS) for c in range(CORES)]
        for h in range(CHIPS)
    ]
    fan = SHARDS * CORES
    spec = jax.ShapeDtypeStruct
    rest = (1, 3, 2)
    small = pltpu.CompilerParams(vmem_limit_bytes=8 * 1024 * 1024)

    spread = pl.pallas_call(
        spread_kernel,
        grid_spec=pltpu.PrefetchScalarGridSpec(
            num_scalar_prefetch=1, grid=(1,),
            in_specs=[whole((tokens, cols))],
            out_specs=pl.BlockSpec(memory_space=pl.ANY),
            scratch_shapes=[pltpu.VMEM((tokens, cols), BF16), pltpu.SemaphoreType.DMA((fan,))],
        ),
        out_shape=spec((fan, tokens, cols), BF16),
        cost_estimate=cost(0, 600_000), name="spread", compiler_params=small,
    )(idx, value_cot)
    cots = lax.all_to_all(
        spread, ("shard", "tensor"), 0, 0, axis_index_groups=near, tiled=True
    )
    other_weight = lax.ppermute(value_weight, "tensor", swap)

    gains = gain.reshape(width // 128, 128)
    part = width // SHARDS
    packing = pl.pallas_call(
        pack_kernel,
        grid_spec=pltpu.PrefetchScalarGridSpec(
            num_scalar_prefetch=1, grid=(tokens // 16,),
            in_specs=[pl.BlockSpec((16, width), lambda i, _: (i, 0)), whole(gains.shape)],
            out_specs=[
                pl.BlockSpec(
                    (SHARDS, 16, part // CORES),
                    lambda i, at: (0, ((i // CORES) ^ at[1]) + CHIPS * (i % CORES), 0),
                ),
            ],
            scratch_shapes=[pltpu.VMEM(gains.shape, F32)],
        ),
        out_shape=[spec((SHARDS, tokens, part // CORES), BF16)],
        cost_estimate=cost(6_000_000, 4_300_000), name="pack", compiler_params=small,
    )
    (sent,) = packing(idx, inputs, gains)
    mine = lax.all_to_all(sent, "shard", 0, 0, tiled=True)
    mine = mine.reshape(SHARDS * tokens, part // CORES)
    theirs = lax.ppermute(mine, "tensor", swap)
    normed = jnp.where(
        tensor % CORES == 0,
        jnp.concatenate([mine, theirs], axis=1),
        jnp.concatenate([theirs, mine], axis=1),
    )

    pairs = cots.reshape(SHARDS, CORES, tokens, cols)
    core = tensor % CORES
    share = tokens // CORES
    own_cots = lax.dynamic_index_in_dim(pairs, core, 1, keepdims=False)

    def half_of(source):
        block = lax.dynamic_slice(
            pairs, (0, source, core * share, 0), (SHARDS, 1, share, cols)
        )
        return block.reshape(SHARDS * share, cols)

    own_rows, other_rows = half_of(core), half_of(1 - core)
    last_dims = (((1,), (1,)), ((), ()))
    product = lax.dot_general(own_rows, value_weight, last_dims, preferred_element_type=F32)
    product += lax.dot_general(other_rows, other_weight, last_dims, preferred_element_type=F32)
    product = product.astype(BF16).reshape(SHARDS, CHIPS, 16, rows)
    outs = [product[:, j].reshape(SHARDS * 16, rows) for j in range(CHIPS)]
    hidden = [outs[0], None, None, None]
    for j in rest:
        hidden[j] = lax.ppermute(outs[j], "tensor", chip_shift(j))

    frows, fcols = pseudo_grad.shape[1:]
    own_cols = fcols // replicas
    outer_packing = pl.pallas_call(
        outer_pack_kernel, grid=(3,),
        in_specs=[pl.BlockSpec((1, frows, fcols // 3), lambda i: (0, 0, i))],
        out_specs=pl.BlockSpec((replicas // 3, frows, own_cols), lambda i: (i, 0, 0)),
        out_shape=spec((replicas, frows, own_cols), BF16),
        cost_estimate=cost(0, 1_200_000), name="outerpack", compiler_params=small,
    )
    packed = outer_packing(pseudo_grad)
    grads = lax.all_to_all(packed, "replica", 0, 0, tiled=True)

    partial_values = jnp.dot(normed, value_weight, preferred_element_type=F32).astype(BF16)
    weight_grad = lax.dot_general(
        normed, own_cots.reshape(SHARDS * tokens, cols),
        (((0,), (0,)), ((), ())), preferred_element_type=F32,
    ).astype(BF16)[None]

    keep, own_values, *merged = pl.pallas_call(
        merge_kernel,
        grid_spec=pltpu.PrefetchScalarGridSpec(
            num_scalar_prefetch=1, grid=(1,),
            in_specs=[whole((64, rows))] * CHIPS + [whole((SHARDS * tokens, cols))],
            out_specs=[whole((16, rows)), whole((tokens, cols))] + [whole((2 * tokens, cols))] * 3,
        ),
        out_shape=[spec((16, rows), F32), spec((tokens, cols), BF16)]
        + [spec((2 * tokens, cols), BF16)] * 3,
        cost_estimate=cost(1_000_000, 1_700_000), name="merge", compiler_params=small,
    )(idx, *hidden, partial_values)
    got = [None] * SHARDS
    for k in rest:
        got[k] = lax.ppermute(merged[k - 1], "shard", shard_shift(k))

    input_grad, values, new_global, new_momentum = pl.pallas_call(
        final_kernel,
        grid_spec=pltpu.PrefetchScalarGridSpec(
            num_scalar_prefetch=1, grid=(1,),
            in_specs=[whole((16, rows))] + [whole((2 * tokens, cols))] * 3
            + [
                whole((tokens, cols)),
                pl.BlockSpec((16, width), lambda i, at: (at[3], 0)),
                whole(gains.shape),
                whole(grads.shape),
                whole(momentum.shape),
                whole(momentum.shape),
            ],
            out_specs=[
                whole((16, width)), whole((tokens, cols)),
                whole(momentum.shape), whole(momentum.shape),
            ],
            scratch_shapes=[pltpu.VMEM(gains.shape, F32)],
        ),
        out_shape=[spec((16, width), BF16), spec((tokens, cols), BF16)]
        + [spec(momentum.shape, F32)] * 2,
        cost_estimate=cost(2_000_000, 2_100_000), name="final", compiler_params=small,
    )(idx, keep, *got[1:], own_values, inputs, gains, grads, global_params, momentum)
    return (values, weight_grad, input_grad, new_global, new_momentum)


def solution(mesh):
    placed = (
        P(("replica", "shard"), None),
        P(),
        P("shard", "tensor"),
        P(("replica", "shard"), "tensor"),
        P("replica", ("shard", "tensor"), None),
        P(("shard", "tensor"), "replica"),
        P(("shard", "tensor"), "replica"),
    )
    return jax.shard_map(
        body,
        mesh=mesh,
        in_specs=placed,
        out_specs=(
            P(("replica", "shard"), "tensor"),
            P("replica", "shard", "tensor"),
            P(("replica", "shard", "tensor"), None),
            P(("shard", "tensor"), "replica"),
            P(("shard", "tensor"), "replica"),
        ),
        check_vma=False,
    )
```

```python
import jax
import jax.numpy as jnp
from jax import lax
from jax.experimental import pallas as pl
from jax.experimental.pallas import tpu as pltpu
from jax.sharding import PartitionSpec as P


norm_epsilon = 1e-05
outer_rate = 0.7
outer_beta = 0.9
CORES = 2
SHARDS = 4
CHIPS = 4
F32 = jnp.float32
BF16 = jnp.bfloat16


def cost(flops, moved):
    return pl.CostEstimate(flops=flops, bytes_accessed=moved, transcendentals=0)


def whole(shape):
    return pl.BlockSpec(shape, lambda *_: (0,) * len(shape))


def block_of(idx, place):
    return CORES * (idx[1] ^ (place % CHIPS)) + place // CHIPS


def spread_kernel(idx, x_ref, o_ref, ordered, sems):
    for place in range(2 * CHIPS):
        at = pl.multiple_of(block_of(idx, place) * 16, 16)
        ordered[place * 16:(place + 1) * 16, :] = x_ref[pl.ds(at, 16), :]
    copies = [
        pltpu.make_async_copy(ordered, o_ref.at[i], sems.at[i]) for i in range(o_ref.shape[0])
    ]
    for copy in copies:
        copy.start()
    for copy in copies:
        copy.wait()


def inverse_scale(x_ref):
    rows, width = x_ref.shape
    total = jnp.zeros((rows, 512), F32)
    for q in range(width // 512):
        wide = x_ref[:, q * 512:(q + 1) * 512].astype(F32)
        total += wide * wide
    inv = lax.rsqrt(jnp.sum(total, axis=1, keepdims=True) / width + norm_epsilon)
    return jnp.broadcast_to(inv, (rows, 128))


def pack_kernel(idx, x_ref, g_ref, o_ref, gain):
    @pl.when(pl.program_id(0) == 0)
    def _():
        gain[...] = g_ref[...].astype(F32)

    width = x_ref.shape[1]
    part = width // SHARDS
    inv = inverse_scale(x_ref)
    half = part // CORES
    for d in range(SHARDS):
        for q in range(half // 128):
            row = (d * CORES + idx[0]) * (half // 128) + q
            wide = x_ref[:, pl.ds(pl.multiple_of(row * 128, 128), 128)].astype(F32)
            o_ref[d, :, q * 128:(q + 1) * 128] = (wide * inv * gain[pl.ds(row, 1), :]).astype(BF16)


def merge_kernel(idx, h0, r1, r2, r3, values, m0, m1, m2, m3):
    cols = m0.shape[1]
    tokens = m0.shape[0] // 2
    for k, out in enumerate((m0, m1, m2, m3)):
        at = pl.ds(pl.multiple_of((idx[2] ^ k) * 16, 16), 16)
        for q in range(h0.shape[1] // cols):
            lanes = slice(q * cols, (q + 1) * cols)
            total = h0[at, lanes].astype(F32) + r1[at, lanes].astype(F32)
            total += r2[at, lanes].astype(F32) + r3[at, lanes].astype(F32)
            out[q * 16:(q + 1) * 16, :] = total.astype(BF16)
        out[tokens:, :] = values[pl.ds(pl.multiple_of((idx[2] ^ k) * tokens, tokens), tokens), :]


def final_kernel(
    idx, m0, m1, m2, m3, x_ref, g_ref, grads, p_ref, q_ref,
    o_ref, val_ref, new_p, new_m, gain,
):
    gain[...] = g_ref[...].astype(F32)
    tokens = val_ref.shape[0]
    cols = m0.shape[1]
    width = x_ref.shape[1]
    part = width // SHARDS
    lanes = 128
    inv = inverse_scale(x_ref)
    places = []
    for k, got in enumerate((m0, m1, m2, m3)):
        first = (idx[2] ^ k) * (part // lanes)
        for q in range(part // lanes):
            at = pl.ds(pl.multiple_of((first + q) * lanes, lanes), lanes)
            places.append((got, q, first + q, at))

    def scaled(got, q, row, at):
        r, l = q * lanes // cols * 16, q * lanes % cols
        return gain[pl.ds(row, 1), :] * got[r:r + 16, l:l + lanes].astype(F32)

    total = jnp.zeros((16, lanes), F32)
    for place in places:
        total += x_ref[:, place[3]].astype(F32) * scaled(*place)
    mean = jnp.sum(total, axis=1, keepdims=True) / width
    factor = inv * inv * inv * mean
    for place in places:
        at = place[3]
        o_ref[:, at] = (inv * scaled(*place) - x_ref[:, at].astype(F32) * factor).astype(BF16)
    for place in range(2 * CHIPS):
        rows = slice(tokens + place * 16, tokens + (place + 1) * 16)
        summed = m0[rows, :].astype(F32)
        for got in (m1, m2, m3):
            summed += got[rows, :].astype(F32)
        to = pl.ds(pl.multiple_of(block_of(idx, place) * 16, 16), 16)
        val_ref[to, :] = summed.astype(BF16)

    replicas = grads.shape[0]
    outer = grads[0].astype(F32)
    for r in range(1, replicas):
        outer += grads[r].astype(F32)
    average = outer / replicas
    momentum = outer_beta * q_ref[...] + average
    new_m[...] = momentum
    new_p[...] = p_ref[...] - outer_rate * (average + outer_beta * momentum)


def outer_pack_kernel(x_ref, o_ref):
    cols = o_ref.shape[2]
    for r in range(o_ref.shape[0]):
        o_ref[r] = x_ref[0, :, r * cols:(r + 1) * cols].astype(BF16)


def body(inputs, gain, value_weight, value_cot, pseudo_grad, global_params, momentum):
    tensors = lax.axis_size("tensor")
    replicas = lax.axis_size("replica")
    tokens, width = inputs.shape
    rows, cols = value_weight.shape
    tensor = lax.axis_index("tensor")
    shard = lax.axis_index("shard")
    idx = jnp.stack([tensor % CORES, tensor // CORES, shard, tensor]).astype(jnp.int32)
    swap = [(i, i ^ 1) for i in range(tensors)]
    chip_shift = lambda j: [
        (t, (t // CORES ^ j) * CORES + t % CORES) for t in range(tensors)
    ]
    shard_shift = lambda k: [(s, s ^ k) for s in range(SHARDS)]
    near = [
        [s * tensors + h * CORES + c for s in range(SHARDS) for c in range(CORES)]
        for h in range(CHIPS)
    ]
    fan = SHARDS * CORES
    spec = jax.ShapeDtypeStruct
    rest = (1, 3, 2)
    small = pltpu.CompilerParams(vmem_limit_bytes=8 * 1024 * 1024)

    spread = pl.pallas_call(
        spread_kernel,
        grid_spec=pltpu.PrefetchScalarGridSpec(
            num_scalar_prefetch=1, grid=(1,),
            in_specs=[whole((tokens, cols))],
            out_specs=pl.BlockSpec(memory_space=pl.ANY),
            scratch_shapes=[pltpu.VMEM((tokens, cols), BF16), pltpu.SemaphoreType.DMA((fan,))],
        ),
        out_shape=spec((fan, tokens, cols), BF16),
        cost_estimate=cost(0, 600_000), name="spread", compiler_params=small,
    )(idx, value_cot)
    cots = lax.all_to_all(
        spread, ("shard", "tensor"), 0, 0, axis_index_groups=near, tiled=True
    )
    other_weight = lax.ppermute(value_weight, "tensor", swap)

    gains = gain.reshape(width // 128, 128)
    part = width // SHARDS
    packing = pl.pallas_call(
        pack_kernel,
        grid_spec=pltpu.PrefetchScalarGridSpec(
            num_scalar_prefetch=1, grid=(tokens // 16,),
            in_specs=[pl.BlockSpec((16, width), lambda i, _: (i, 0)), whole(gains.shape)],
            out_specs=[
                pl.BlockSpec(
                    (SHARDS, 16, part // CORES),
                    lambda i, at: (0, ((i // CORES) ^ at[1]) + CHIPS * (i % CORES), 0),
                ),
            ],
            scratch_shapes=[pltpu.VMEM(gains.shape, F32)],
        ),
        out_shape=[spec((SHARDS, tokens, part // CORES), BF16)],
        cost_estimate=cost(6_000_000, 4_300_000), name="pack", compiler_params=small,
    )
    (sent,) = packing(idx, inputs, gains)
    mine = lax.all_to_all(sent, "shard", 0, 0, tiled=True)
    mine = mine.reshape(SHARDS * tokens, part // CORES)
    theirs = lax.ppermute(mine, "tensor", swap)
    normed = jnp.where(
        tensor % CORES == 0,
        jnp.concatenate([mine, theirs], axis=1),
        jnp.concatenate([theirs, mine], axis=1),
    )

    pairs = cots.reshape(SHARDS, CORES, tokens, cols)
    core = tensor % CORES
    share = tokens // CORES
    own_cots = lax.dynamic_index_in_dim(pairs, core, 1, keepdims=False)

    def half_of(source):
        block = lax.dynamic_slice(
            pairs, (0, source, core * share, 0), (SHARDS, 1, share, cols)
        )
        return block.reshape(SHARDS * share, cols)

    own_rows, other_rows = half_of(core), half_of(1 - core)
    last_dims = (((1,), (1,)), ((), ()))
    product = lax.dot_general(own_rows, value_weight, last_dims, preferred_element_type=F32)
    product += lax.dot_general(other_rows, other_weight, last_dims, preferred_element_type=F32)
    product = product.astype(BF16).reshape(SHARDS, CHIPS, 16, rows)
    outs = [product[:, j].reshape(SHARDS * 16, rows) for j in range(CHIPS)]
    hidden = [outs[0], None, None, None]
    for j in rest:
        hidden[j] = lax.ppermute(outs[j], "tensor", chip_shift(j))

    frows, fcols = pseudo_grad.shape[1:]
    own_cols = fcols // replicas
    outer_packing = pl.pallas_call(
        outer_pack_kernel, grid=(3,),
        in_specs=[pl.BlockSpec((1, frows, fcols // 3), lambda i: (0, 0, i))],
        out_specs=pl.BlockSpec((replicas // 3, frows, own_cols), lambda i: (i, 0, 0)),
        out_shape=spec((replicas, frows, own_cols), BF16),
        cost_estimate=cost(0, 1_200_000), name="outerpack", compiler_params=small,
    )
    packed = outer_packing(pseudo_grad)
    grads = lax.all_to_all(packed, "replica", 0, 0, tiled=True)

    partial_values = jnp.dot(normed, value_weight, preferred_element_type=F32).astype(BF16)
    weight_grad = lax.dot_general(
        normed, own_cots.reshape(SHARDS * tokens, cols),
        (((0,), (0,)), ((), ())), preferred_element_type=F32,
    ).astype(BF16)[None]

    merged = pl.pallas_call(
        merge_kernel,
        grid_spec=pltpu.PrefetchScalarGridSpec(
            num_scalar_prefetch=1, grid=(1,),
            in_specs=[whole((64, rows))] * CHIPS + [whole((SHARDS * tokens, cols))],
            out_specs=[whole((2 * tokens, cols))] * SHARDS,
        ),
        out_shape=[spec((2 * tokens, cols), BF16)] * SHARDS,
        cost_estimate=cost(1_000_000, 1_700_000), name="merge", compiler_params=small,
    )(idx, *hidden, partial_values)
    got = [merged[0], None, None, None]
    for k in rest:
        got[k] = lax.ppermute(merged[k], "shard", shard_shift(k))

    input_grad, values, new_global, new_momentum = pl.pallas_call(
        final_kernel,
        grid_spec=pltpu.PrefetchScalarGridSpec(
            num_scalar_prefetch=1, grid=(1,),
            in_specs=[whole((2 * tokens, cols))] * SHARDS
            + [
                pl.BlockSpec((16, width), lambda i, at: (at[3], 0)),
                whole(gains.shape),
                whole(grads.shape),
                whole(momentum.shape),
                whole(momentum.shape),
            ],
            out_specs=[
                whole((16, width)), whole((tokens, cols)),
                whole(momentum.shape), whole(momentum.shape),
            ],
            scratch_shapes=[pltpu.VMEM(gains.shape, F32)],
        ),
        out_shape=[spec((16, width), BF16), spec((tokens, cols), BF16)]
        + [spec(momentum.shape, F32)] * 2,
        cost_estimate=cost(2_000_000, 2_100_000), name="final", compiler_params=small,
    )(idx, *got, inputs, gains, grads, global_params, momentum)
    return (values, weight_grad, input_grad, new_global, new_momentum)


def solution(mesh):
    placed = (
        P(("replica", "shard"), None),
        P(),
        P("shard", "tensor"),
        P(("replica", "shard"), "tensor"),
        P("replica", ("shard", "tensor"), None),
        P(("shard", "tensor"), "replica"),
        P(("shard", "tensor"), "replica"),
    )
    return jax.shard_map(
        body,
        mesh=mesh,
        in_specs=placed,
        out_specs=(
            P(("replica", "shard"), "tensor"),
            P("replica", "shard", "tensor"),
            P(("replica", "shard", "tensor"), None),
            P(("shard", "tensor"), "replica"),
            P(("shard", "tensor"), "replica"),
        ),
        check_vma=False,
    )
```

```python
import jax
import jax.numpy as jnp
from jax import lax
from jax.experimental import pallas as pl
from jax.experimental.pallas import tpu as pltpu
from jax.sharding import PartitionSpec as P


norm_epsilon = 1e-05
outer_rate = 0.7
outer_beta = 0.9
CORES = 2
SHARDS = 4
CHIPS = 4
F32 = jnp.float32
BF16 = jnp.bfloat16


def cost(flops, moved):
    return pl.CostEstimate(flops=flops, bytes_accessed=moved, transcendentals=0)


def whole(shape):
    return pl.BlockSpec(shape, lambda *_: (0,) * len(shape))


def block_of(idx, place):
    return CORES * (idx[1] ^ (place % CHIPS)) + place // CHIPS


def spread_kernel(idx, x_ref, o_ref, ordered, sems):
    for place in range(2 * CHIPS):
        at = pl.multiple_of(block_of(idx, place) * 16, 16)
        ordered[place * 16:(place + 1) * 16, :] = x_ref[pl.ds(at, 16), :]
    copies = [
        pltpu.make_async_copy(ordered, o_ref.at[i], sems.at[i]) for i in range(o_ref.shape[0])
    ]
    for copy in copies:
        copy.start()
    for copy in copies:
        copy.wait()


def inverse_scale(x_ref):
    rows, width = x_ref.shape
    total = jnp.zeros((rows, 512), F32)
    for q in range(width // 512):
        wide = x_ref[:, q * 512:(q + 1) * 512].astype(F32)
        total += wide * wide
    inv = lax.rsqrt(jnp.sum(total, axis=1, keepdims=True) / width + norm_epsilon)
    return jnp.broadcast_to(inv, (rows, 128))


def pack_kernel(idx, x_ref, g_ref, o_ref, gain):
    @pl.when(pl.program_id(0) == 0)
    def _():
        gain[...] = g_ref[...].astype(F32)

    width = x_ref.shape[1]
    part = width // SHARDS
    inv = inverse_scale(x_ref)
    half = part // CORES
    for d in range(SHARDS):
        for q in range(half // 128):
            row = (d * CORES + idx[0]) * (half // 128) + q
            wide = x_ref[:, pl.ds(pl.multiple_of(row * 128, 128), 128)].astype(F32)
            o_ref[d, :, q * 128:(q + 1) * 128] = (wide * inv * gain[pl.ds(row, 1), :]).astype(BF16)


def merge_kernel(idx, h0, r1, r2, r3, values, m0, m1, m2, m3):
    cols = m0.shape[1]
    tokens = m0.shape[0] // 2
    for k, out in enumerate((m0, m1, m2, m3)):
        at = pl.ds(pl.multiple_of((idx[2] ^ k) * 16, 16), 16)
        for q in range(h0.shape[1] // cols):
            lanes = slice(q * cols, (q + 1) * cols)
            total = h0[at, lanes].astype(F32) + r1[at, lanes].astype(F32)
            total += r2[at, lanes].astype(F32) + r3[at, lanes].astype(F32)
            out[q * 16:(q + 1) * 16, :] = total.astype(BF16)
        out[tokens:, :] = values[pl.ds(pl.multiple_of((idx[2] ^ k) * tokens, tokens), tokens), :]


def final_kernel(
    idx, m0, m1, m2, m3, x_ref, g_ref, grads, p_ref, q_ref,
    o_ref, val_ref, new_p, new_m, gain,
):
    gain[...] = g_ref[...].astype(F32)
    tokens = val_ref.shape[0]
    cols = m0.shape[1]
    width = x_ref.shape[1]
    part = width // SHARDS
    lanes = 128
    inv = inverse_scale(x_ref)
    places = []
    for k, got in enumerate((m0, m1, m2, m3)):
        first = (idx[2] ^ k) * (part // lanes)
        for q in range(part // lanes):
            at = pl.ds(pl.multiple_of((first + q) * lanes, lanes), lanes)
            places.append((got, q, first + q, at))

    def scaled(got, q, row, at):
        r, l = q * lanes // cols * 16, q * lanes % cols
        return gain[pl.ds(row, 1), :] * got[r:r + 16, l:l + lanes].astype(F32)

    total = jnp.zeros((16, lanes), F32)
    for place in places:
        total += x_ref[:, place[3]].astype(F32) * scaled(*place)
    mean = jnp.sum(total, axis=1, keepdims=True) / width
    factor = inv * inv * inv * mean
    for place in places:
        at = place[3]
        o_ref[:, at] = (inv * scaled(*place) - x_ref[:, at].astype(F32) * factor).astype(BF16)
    for place in range(2 * CHIPS):
        rows = slice(tokens + place * 16, tokens + (place + 1) * 16)
        summed = m0[rows, :].astype(F32)
        for got in (m1, m2, m3):
            summed += got[rows, :].astype(F32)
        to = pl.ds(pl.multiple_of(block_of(idx, place) * 16, 16), 16)
        val_ref[to, :] = summed.astype(BF16)

    replicas = grads.shape[0]
    outer = grads[0].astype(F32)
    for r in range(1, replicas):
        outer += grads[r].astype(F32)
    average = outer / replicas
    momentum = outer_beta * q_ref[...] + average
    new_m[...] = momentum
    new_p[...] = p_ref[...] - outer_rate * (average + outer_beta * momentum)


def outer_pack_kernel(x_ref, o_ref):
    cols = o_ref.shape[2]
    for r in range(o_ref.shape[0]):
        o_ref[r] = x_ref[0, :, r * cols:(r + 1) * cols].astype(BF16)


def body(inputs, gain, value_weight, value_cot, pseudo_grad, global_params, momentum):
    tensors = lax.axis_size("tensor")
    replicas = lax.axis_size("replica")
    tokens, width = inputs.shape
    rows, cols = value_weight.shape
    tensor = lax.axis_index("tensor")
    shard = lax.axis_index("shard")
    idx = jnp.stack([tensor % CORES, tensor // CORES, shard, tensor]).astype(jnp.int32)
    swap = [(i, i ^ 1) for i in range(tensors)]
    chip_shift = lambda j: [
        (t, (t // CORES ^ j) * CORES + t % CORES) for t in range(tensors)
    ]
    shard_shift = lambda k: [(s, s ^ k) for s in range(SHARDS)]
    near = [
        [s * tensors + h * CORES + c for s in range(SHARDS) for c in range(CORES)]
        for h in range(CHIPS)
    ]
    fan = SHARDS * CORES
    spec = jax.ShapeDtypeStruct
    rest = (1, 3, 2)
    small = pltpu.CompilerParams(vmem_limit_bytes=8 * 1024 * 1024)

    spread = pl.pallas_call(
        spread_kernel,
        grid_spec=pltpu.PrefetchScalarGridSpec(
            num_scalar_prefetch=1, grid=(1,),
            in_specs=[whole((tokens, cols))],
            out_specs=pl.BlockSpec(memory_space=pl.ANY),
            scratch_shapes=[pltpu.VMEM((tokens, cols), BF16), pltpu.SemaphoreType.DMA((fan,))],
        ),
        out_shape=spec((fan, tokens, cols), BF16),
        cost_estimate=cost(0, 600_000), name="spread", compiler_params=small,
    )(idx, value_cot)
    cots = lax.all_to_all(
        spread, ("shard", "tensor"), 0, 0, axis_index_groups=near, tiled=True
    )
    other_weight = lax.ppermute(value_weight, "tensor", swap)

    gains = gain.reshape(width // 128, 128)
    part = width // SHARDS
    packing = pl.pallas_call(
        pack_kernel,
        grid_spec=pltpu.PrefetchScalarGridSpec(
            num_scalar_prefetch=1, grid=(tokens // 16,),
            in_specs=[pl.BlockSpec((16, width), lambda i, _: (i, 0)), whole(gains.shape)],
            out_specs=[
                pl.BlockSpec(
                    (SHARDS, 16, part // CORES),
                    lambda i, at: (0, ((i // CORES) ^ at[1]) + CHIPS * (i % CORES), 0),
                ),
            ],
            scratch_shapes=[pltpu.VMEM(gains.shape, F32)],
        ),
        out_shape=[spec((SHARDS, tokens, part // CORES), BF16)],
        cost_estimate=cost(6_000_000, 4_300_000), name="pack", compiler_params=small,
    )
    (sent,) = packing(idx, inputs, gains)
    mine = lax.all_to_all(sent, "shard", 0, 0, tiled=True)
    mine = mine.reshape(SHARDS * tokens, part // CORES)
    theirs = lax.ppermute(mine, "tensor", swap)
    normed = jnp.where(
        tensor % CORES == 0,
        jnp.concatenate([mine, theirs], axis=1),
        jnp.concatenate([theirs, mine], axis=1),
    )

    pairs = cots.reshape(SHARDS, CORES, tokens, cols)
    core = tensor % CORES
    share = tokens // CORES
    own_cots = lax.dynamic_index_in_dim(pairs, core, 1, keepdims=False)

    def half_of(source):
        block = lax.dynamic_slice(
            pairs, (0, source, core * share, 0), (SHARDS, 1, share, cols)
        )
        return block.reshape(SHARDS * share, cols)

    own_rows, other_rows = half_of(core), half_of(1 - core)
    last_dims = (((1,), (1,)), ((), ()))
    product = lax.dot_general(
        jnp.concatenate([own_rows, other_rows], axis=1),
        jnp.concatenate([value_weight, other_weight], axis=1),
        last_dims, preferred_element_type=F32,
    )
    product = product.astype(BF16).reshape(SHARDS, CHIPS, 16, rows)
    outs = [product[:, j].reshape(SHARDS * 16, rows) for j in range(CHIPS)]
    hidden = [outs[0], None, None, None]
    for j in rest:
        hidden[j] = lax.ppermute(outs[j], "tensor", chip_shift(j))

    frows, fcols = pseudo_grad.shape[1:]
    own_cols = fcols // replicas
    outer_packing = pl.pallas_call(
        outer_pack_kernel, grid=(3,),
        in_specs=[pl.BlockSpec((1, frows, fcols // 3), lambda i: (0, 0, i))],
        out_specs=pl.BlockSpec((replicas // 3, frows, own_cols), lambda i: (i, 0, 0)),
        out_shape=spec((replicas, frows, own_cols), BF16),
        cost_estimate=cost(0, 1_200_000), name="outerpack", compiler_params=small,
    )
    packed = outer_packing(pseudo_grad)
    grads = lax.all_to_all(packed, "replica", 0, 0, tiled=True)

    halves = value_weight.reshape(CORES, rows // CORES, cols)
    partial_values = jnp.dot(
        mine, lax.dynamic_index_in_dim(halves, core, 0, keepdims=False), preferred_element_type=F32
    )
    partial_values += jnp.dot(
        theirs, lax.dynamic_index_in_dim(halves, 1 - core, 0, keepdims=False),
        preferred_element_type=F32,
    )
    partial_values = partial_values.astype(BF16)
    weight_grad = lax.dot_general(
        normed, own_cots.reshape(SHARDS * tokens, cols),
        (((0,), (0,)), ((), ())), preferred_element_type=F32,
    ).astype(BF16)[None]

    merged = pl.pallas_call(
        merge_kernel,
        grid_spec=pltpu.PrefetchScalarGridSpec(
            num_scalar_prefetch=1, grid=(1,),
            in_specs=[whole((64, rows))] * CHIPS + [whole((SHARDS * tokens, cols))],
            out_specs=[whole((2 * tokens, cols))] * SHARDS,
        ),
        out_shape=[spec((2 * tokens, cols), BF16)] * SHARDS,
        cost_estimate=cost(1_000_000, 1_700_000), name="merge", compiler_params=small,
    )(idx, *hidden, partial_values)
    got = [merged[0], None, None, None]
    for k in rest:
        got[k] = lax.ppermute(merged[k], "shard", shard_shift(k))

    input_grad, values, new_global, new_momentum = pl.pallas_call(
        final_kernel,
        grid_spec=pltpu.PrefetchScalarGridSpec(
            num_scalar_prefetch=1, grid=(1,),
            in_specs=[whole((2 * tokens, cols))] * SHARDS
            + [
                pl.BlockSpec((16, width), lambda i, at: (at[3], 0)),
                whole(gains.shape),
                whole(grads.shape),
                whole(momentum.shape),
                whole(momentum.shape),
            ],
            out_specs=[
                whole((16, width)), whole((tokens, cols)),
                whole(momentum.shape), whole(momentum.shape),
            ],
            scratch_shapes=[pltpu.VMEM(gains.shape, F32)],
        ),
        out_shape=[spec((16, width), BF16), spec((tokens, cols), BF16)]
        + [spec(momentum.shape, F32)] * 2,
        cost_estimate=cost(2_000_000, 2_100_000), name="final", compiler_params=small,
    )(idx, *got, inputs, gains, grads, global_params, momentum)
    return (values, weight_grad, input_grad, new_global, new_momentum)


def solution(mesh):
    placed = (
        P(("replica", "shard"), None),
        P(),
        P("shard", "tensor"),
        P(("replica", "shard"), "tensor"),
        P("replica", ("shard", "tensor"), None),
        P(("shard", "tensor"), "replica"),
        P(("shard", "tensor"), "replica"),
    )
    return jax.shard_map(
        body,
        mesh=mesh,
        in_specs=placed,
        out_specs=(
            P(("replica", "shard"), "tensor"),
            P("replica", "shard", "tensor"),
            P(("replica", "shard", "tensor"), None),
            P(("shard", "tensor"), "replica"),
            P(("shard", "tensor"), "replica"),
        ),
        check_vma=False,
    )
```
